32 devices in a mesh: wide: 8 (over z, x), narrow: 4 (over y, core).
Axes of the slice: x: 2, y: 2, z: 4, core: 2. Of those that a mesh axis runs over, the one named last changes fastest.
Arguments:
- embeddings: bfloat16 [16384, 1024], P(('wide', 'narrow')), may hold values from -32 to 32
- valid: int32 [16384], P(('wide', 'narrow')), may hold values from 0 to 1, as said below
Outputs:
- whitened: bfloat16 [16384, 1024], P(('wide', 'narrow'))
The draws below stay inside these ranges and needn't reach their ends.
Inputs may be any that keep to these rules, and one draw needn't show every extreme that they name: The first row of every aligned block of 16 rows has valid = 1.
All inputs are finite; a program needn't handle non-finite values.
Results may differ from the reference program's by a relative error of at most 0.001.
Values sent between devices are 32-bit elements; how exact they have to be, the bound alone decides.
No kernel may reach another device: no remote copies, remote signals or barrier semaphores. Data moves between devices by JAX's collectives and lax.ppermute only.
A program may use at most 64 MiB of HBM per device.

```python
import math
import jax
import jax.numpy as jnp
from jax import lax

D = 1024
ITERS = 2
ROWS = 16384
N_WIDE = 8


def draw_embeddings(key, part):
    keys = jax.random.split(key, 4)
    col_scale = jnp.exp(jax.random.uniform(keys[0], (D,), jnp.float32, 0.0, math.log(10.0))) / 3.0
    col_mean = 1.5 * jax.random.normal(keys[1], (D,), jnp.float32)
    drift = jax.random.normal(keys[2], (D,), jnp.float32)
    position = (jnp.arange(ROWS, dtype=jnp.float32) / ROWS)[:, None]
    noise = jax.random.normal(keys[3], (ROWS, D), jnp.float32)
    values = noise * col_scale + col_mean + 1.5 * position * drift
    return jnp.clip(values, -32.0, 32.0).astype(jnp.bfloat16)


def draw_valid(key, part):
    index = jnp.arange(ROWS, dtype=jnp.int32)
    ticket = jax.random.randint(jax.random.fold_in(key, 7), (ROWS,), 0, 1000, jnp.int32)
    threshold = 250 + 650 * index // ROWS
    chosen = jnp.logical_or(ticket < threshold, index % 16 == 0)
    return chosen.astype(jnp.int32)


def setup_inputs(seed: int = 0) -> dict:
    streams_of = jax.random.split(jax.random.key(seed), 3)
    embeddings = draw_embeddings(jax.random.fold_in(streams_of[2], 71), 0)
    valid = draw_valid(jax.random.fold_in(streams_of[2], 71), 0)
    return dict(embeddings=embeddings, valid=valid)


def reference(embeddings, valid):
    mask_half = valid.astype(jnp.bfloat16)
    count = jnp.sum(valid.astype(jnp.float32))
    blocks_x = embeddings.reshape(N_WIDE, -1, D)
    blocks_m = mask_half.reshape(N_WIDE, -1)

    def accumulate(state, item):
        gram, sums = state
        block_x, block_m = item
        masked = block_x * block_m[:, None]
        gram = gram + lax.dot_general(masked, block_x, (((0,), (0,)), ((), ())), preferred_element_type=jnp.float32)
        sums = sums + jnp.dot(block_m[None, :], block_x, preferred_element_type=jnp.float32)[0]
        return ((gram, sums), None)
    start_state = (jnp.zeros((D, D), jnp.float32), jnp.zeros((D,), jnp.float32))
    (gram, sums), _ = lax.scan(accumulate, start_state, (blocks_x, blocks_m))
    center = sums / count
    scatter = gram - sums[:, None] * center[None, :] - center[:, None] * sums[None, :] + count * center[:, None] * center[None, :]
    cov = scatter / count
    trace_cov = jnp.trace(cov)
    square_sum = jnp.sum(cov * cov)
    ridge_add = 0.05 * trace_cov / D + 1e-06
    norm_frob = jnp.sqrt(square_sum + 2.0 * ridge_add * trace_cov + D * ridge_add * ridge_add)
    identity = jnp.eye(D, dtype=jnp.float32)
    base = (cov + ridge_add * identity) / norm_frob
    root = (3.0 * identity - base) / 2.0
    for _ in range(ITERS - 1):
        first = jnp.dot(base, root, precision=lax.Precision.HIGHEST, preferred_element_type=jnp.float32)
        second = jnp.dot(first, root, precision=lax.Precision.HIGHEST, preferred_element_type=jnp.float32)
        factor = (3.0 * identity - second) / 2.0
        root = jnp.dot(factor, root, precision=lax.Precision.HIGHEST, preferred_element_type=jnp.float32)

    def whiten_block(block_x):
        shifted = block_x.astype(jnp.float32) - center
        product = jnp.dot(shifted, root, precision=lax.Precision.HIGHEST, preferred_element_type=jnp.float32)
        return (product / jnp.sqrt(norm_frob)).astype(jnp.bfloat16)
    return lax.map(whiten_block, blocks_x).reshape(ROWS, D)
```

```python
import functools

import jax
import jax.numpy as jnp
from jax import lax
from jax.experimental import pallas as pl
from jax.experimental.pallas import tpu as pltpu
from jax.sharding import PartitionSpec as P

AXES = ("wide", "narrow")
BLOCK = 128
LANES = 128
TILE = 8


class Plan:
    def __init__(self, mesh, width):
        wide, narrow = mesh.shape["wide"], mesh.shape["narrow"]
        self.devices = wide * narrow
        narrow_bits = [1 << k for k in range(narrow.bit_length() - 1)]
        wide_bits = [narrow << k for k in range(wide.bit_length() - 1)]
        rest = wide_bits[1:] + narrow_bits[2:]
        stages = [narrow_bits[:1], wide_bits[:1] + narrow_bits[1:2]]
        stages += [list(reversed(rest[k : k + 2])) for k in range(0, len(rest), 2)]
        self.stages = stages
        self.bits = [bit for stage in stages for bit in stage]
        self.count = width // BLOCK
        tiles = self.count * (self.count + 1) // 2 * (BLOCK // TILE)
        self.chunk = -(-tiles // self.devices) * TILE
        self.rows = self.chunk * self.devices
        self.pieces = 1
        for stage in stages[:2]:
            self.pieces <<= len(stage)
        self.subs = self.devices // self.pieces

    def place(self):
        me = lax.axis_index("wide") * lax.axis_size("narrow") + lax.axis_index("narrow")
        place = me * 0
        for bit in self.bits:
            place = place * 2 + (me // bit) % 2
        return place

    def mask(self, stage, digit):
        bits = self.stages[stage]
        return sum(bit for k, bit in enumerate(bits) if (digit >> (len(bits) - 1 - k)) & 1)

    def send(self, value, stage, digit):
        mask = self.mask(stage, digit)
        return lax.ppermute(value, AXES, [(i, i ^ mask) for i in range(self.devices)])

    def block_row(self, i, j):
        return (i * self.count - i * (i - 1) // 2 + (j - i)) * BLOCK


def each_slot(plan, place, go):
    for piece in range(plan.pieces):

        def one(sub, carry, piece=piece):
            go(piece, sub, lax.bitwise_xor(place, piece * plan.subs + sub))
            return carry

        if plan.subs <= 8:
            for sub in range(plan.subs):
                one(sub, 0)
        else:
            lax.fori_loop(0, plan.subs, one, 0)


def gram_kernel(plan, x_ref, valid_ref, *refs):
    outs, (packed, sem) = refs[: plan.pieces], refs[plan.pieces :]
    place = plan.place()
    count = plan.count
    mask = valid_ref[...].astype(jnp.float32)
    mask_half = mask.astype(jnp.bfloat16)
    number = jnp.sum(mask)
    sums = jnp.dot(
        jnp.broadcast_to(mask_half, (16, mask.shape[1])), x_ref[...], preferred_element_type=jnp.float32
    )
    row = lax.broadcasted_iota(jnp.int32, (BLOCK, LANES), 0)
    lane = lax.broadcasted_iota(jnp.int32, (BLOCK, LANES), 1)
    for i in range(0, count, 2):
        left = x_ref[:, i * BLOCK : (i + 2) * BLOCK].T * mask_half
        part = jnp.dot(left, x_ref[:, i * BLOCK :], preferred_element_type=jnp.float32)
        for a in range(2):
            for j in range(i + a, count):
                block = part[a * BLOCK : (a + 1) * BLOCK, (j - i) * BLOCK : (j - i + 1) * BLOCK]
                if j == i + a:
                    s = sums[0:1, j * BLOCK : (j + 1) * BLOCK]
                    turned = jnp.where(lane[0:1] == 0, pltpu.roll(s, 1, 1), number)
                    low = jnp.where(row == BLOCK - 1, s, turned)
                    block = jnp.where(row <= lane, block, low)
                start = plan.block_row(i + a, j)
                packed[start : start + BLOCK, :] = block
    if plan.rows > plan.block_row(count, count):
        start = plan.block_row(count, count)
        packed[start:, :] = jnp.zeros((plan.rows - start, LANES), jnp.float32)

    def copy(piece, sub, source):
        return pltpu.make_async_copy(
            packed.at[pl.ds(pl.multiple_of(source * plan.chunk, TILE), plan.chunk)],
            outs[piece].at[pl.ds(pl.multiple_of(sub * plan.chunk, TILE), plan.chunk)],
            sem,
        )

    each_slot(plan, place, lambda *slot: copy(*slot).start())
    each_slot(plan, place, lambda *slot: copy(*slot).wait())


def gram_pieces(plan, x, valid):
    shape = jax.ShapeDtypeStruct((plan.subs * plan.chunk, LANES), jnp.float32)
    return pl.pallas_call(
        functools.partial(gram_kernel, plan),
        out_shape=[shape] * plan.pieces,
        in_specs=[pl.BlockSpec(memory_space=pltpu.VMEM)] * 2,
        out_specs=[pl.BlockSpec(memory_space=pl.ANY)] * plan.pieces,
        scratch_shapes=[pltpu.VMEM((plan.rows, LANES), jnp.float32), pltpu.SemaphoreType.DMA],
        compiler_params=pltpu.CompilerParams(vmem_limit_bytes=24 << 20),
        name="gram",
    )(x, valid.reshape(1, -1))


def whiten_kernel(plan, x_ref, *refs):
    pieces = refs[: plan.pieces]
    o_ref, packed, high, low, value, half_a, rest_a, half_b, rest_b, sem = refs[plan.pieces :]
    place = plan.place()
    count = plan.count
    width = x_ref.shape[1]

    def copy(piece, sub, source):
        return pltpu.make_async_copy(
            pieces[piece].at[pl.ds(pl.multiple_of(sub * plan.chunk, TILE), plan.chunk)],
            packed.at[pl.ds(pl.multiple_of(source * plan.chunk, TILE), plan.chunk)],
            sem,
        )

    each_slot(plan, place, lambda *slot: copy(*slot).start())
    each_slot(plan, place, lambda *slot: copy(*slot).wait())

    row = lax.broadcasted_iota(jnp.int32, (BLOCK, LANES), 0)
    lane = lax.broadcasted_iota(jnp.int32, (BLOCK, LANES), 1)
    number = packed[BLOCK - 2 : BLOCK - 1, 1:2]
    inverse = 1.0 / number
    centers, columns = [], []
    for i in range(count):
        start = plan.block_row(i, i)
        last = packed[start + BLOCK - 1 : start + BLOCK, :]
        turned = pltpu.roll(packed[start + BLOCK - 2 : start + BLOCK - 1, :], LANES - 1, 1)
        center = jnp.where(lane[0:1] < LANES - 1, last, turned) * inverse
        centers.append(center)
        columns.append(jnp.broadcast_to(center, (BLOCK, LANES)).T)

    def split(cov):
        top = cov.astype(jnp.bfloat16)
        return top, (cov - top.astype(jnp.float32)).astype(jnp.bfloat16)

    trace = jnp.zeros((BLOCK, LANES), jnp.float32)
    square_diag = jnp.zeros((BLOCK, LANES), jnp.float32)
    square_off = jnp.zeros((BLOCK, LANES), jnp.float32)
    for i in range(count):
        for j in range(i, count):
            start = plan.block_row(i, j)
            block = packed[start : start + BLOCK, :]
            if i == j:
                block = jnp.where(row <= lane, block, block.T)
            cov = block * inverse - columns[i] * centers[j]
            if i == j:
                trace += jnp.where(row == lane, cov, 0.0)
                square_diag += cov * cov
            else:
                square_off += cov * cov
            rows, cols = pl.ds(i * BLOCK, BLOCK), pl.ds(j * BLOCK, BLOCK)
            high[rows, cols], low[rows, cols] = split(cov)
            if i != j:
                high[cols, rows], low[cols, rows] = split(cov.T)
    trace = jnp.sum(trace)
    square = jnp.sum(square_diag + 2.0 * square_off)
    ridge = 0.05 * trace / width + 1e-06
    norm = jnp.sqrt(jnp.full((1, 1), square + 2.0 * ridge * trace + width * ridge * ridge, jnp.float32))
    unit = 1.0 / norm
    final = 1.0 / (16.0 * jnp.sqrt(norm))

    step = 2 * BLOCK
    for j in range(count // 2):
        cols = pl.ds(j * step, step)
        center = jnp.concatenate(centers[2 * j : 2 * j + 2], axis=1)
        y = x_ref[:, cols].astype(jnp.float32) - center
        value[:, cols] = y
        half_a[:, cols], rest_a[:, cols] = split(y)

    halves = [(half_a, rest_a), (half_b, rest_b)]
    for k, weight in enumerate((-9.0, 27.0, -39.0, 36.0)):
        (half, rest), (half_next, rest_next) = halves[k % 2], halves[1 - k % 2]
        for j in range(count // 2):
            cols = pl.ds(j * step, step)
            center = jnp.concatenate(centers[2 * j : 2 * j + 2], axis=1)
            product = (
                jnp.dot(half[...], high[:, cols], preferred_element_type=jnp.float32)
                + jnp.dot(half[...], low[:, cols], preferred_element_type=jnp.float32)
                + jnp.dot(rest[...], high[:, cols], preferred_element_type=jnp.float32)
            )
            y = x_ref[:, cols].astype(jnp.float32) - center
            new = (product + ridge * value[:, cols]) * unit + weight * y
            if k < 3:
                value[:, cols] = new
                half_next[:, cols], rest_next[:, cols] = split(new)
            else:
                o_ref[:, cols] = (new * final).astype(jnp.bfloat16)


def whiten(plan, x, pieces):
    rows, width = x.shape
    half = pltpu.VMEM((rows, width), jnp.bfloat16)
    return pl.pallas_call(
        functools.partial(whiten_kernel, plan),
        out_shape=jax.ShapeDtypeStruct(x.shape, jnp.bfloat16),
        in_specs=[pl.BlockSpec(memory_space=pltpu.VMEM)] + [pl.BlockSpec(memory_space=pl.ANY)] * plan.pieces,
        out_specs=pl.BlockSpec(memory_space=pltpu.VMEM),
        scratch_shapes=[
            pltpu.VMEM((plan.rows, LANES), jnp.float32),
            pltpu.VMEM((width, width), jnp.bfloat16),
            pltpu.VMEM((width, width), jnp.bfloat16),
            pltpu.VMEM((rows, width), jnp.float32),
            half,
            half,
            half,
            half,
            pltpu.SemaphoreType.DMA,
        ],
        compiler_params=pltpu.CompilerParams(vmem_limit_bytes=40 << 20),
        name="whiten",
    )(x, *pieces)


def on_device(plan, embeddings, valid):
    pieces = gram_pieces(plan, embeddings, valid)
    fan = plan.pieces // 2
    near = {}
    for digit in reversed(range(fan)):
        near[digit] = pieces[digit] + plan.send(pieces[fan + digit], 0, 1)
    total = near[0]
    for digit in reversed(range(1, fan)):
        total = total + plan.send(near[digit], 1, digit)
    for stage in range(2, len(plan.stages)):
        size = 1 << len(plan.stages[stage])
        span = total.shape[0] // size
        parts = [total[k * span : (k + 1) * span] for k in range(size)]
        total = parts[0]
        for digit in (2, 3, 1)[: size - 1] if size == 4 else (1,):
            total = total + plan.send(parts[digit], stage, digit)
    for stage in reversed(range(2, len(plan.stages))):
        size = 1 << len(plan.stages[stage])
        parts = {0: total}
        for digit in (2, 3, 1)[: size - 1] if size == 4 else (1,):
            parts[digit] = plan.send(total, stage, digit)
        total = jnp.concatenate([parts[k] for k in range(size)], axis=0)
    near = {0: total}
    far = {0: plan.send(total, 0, 1)}
    for digit in reversed(range(1, fan)):
        near[digit] = plan.send(total, 1, digit)
    for digit in reversed(range(1, fan)):
        far[digit] = plan.send(near[digit], 0, 1)
    pieces = [near[k] for k in range(fan)] + [far[k] for k in range(fan)]
    return whiten(plan, embeddings, pieces)


def solution(mesh):
    spec = P(AXES, None)

    def program(embeddings, valid):
        plan = Plan(mesh, embeddings.shape[1])
        body = functools.partial(on_device, plan)
        return jax.shard_map(
            body, mesh=mesh, in_specs=(spec, P(AXES)), out_specs=spec, check_vma=False
        )(embeddings, valid)

    return program
```

```python
import functools

import jax
import jax.numpy as jnp
from jax import lax
from jax.experimental import pallas as pl
from jax.experimental.pallas import tpu as pltpu
from jax.sharding import PartitionSpec as P

AXES = ("wide", "narrow")
BLOCK = 128
LANES = 128
TILE = 8
SHARE = 0.5


class Plan:
    def __init__(self, mesh, width):
        wide, narrow = mesh.shape["wide"], mesh.shape["narrow"]
        self.devices = wide * narrow
        narrow_bits = [1 << k for k in range(1, narrow.bit_length() - 1)]
        wide_bits = [narrow << k for k in range(wide.bit_length() - 1)]
        rest = wide_bits[1:] + narrow_bits[1:]
        plane = [(bit, (bit,)) for bit in wide_bits[:1] + narrow_bits[:1]]
        around = [(rest[0], (rest[0], rest[1])), (rest[0] + rest[1], (rest[1],))]
        others = [[(bit, (bit,)) for bit in rest[k : k + 2]] for k in range(2, len(rest), 2)]
        orders = [[plane, around] + others, [around, plane] + others]
        self.orders = [
            [[dim for group in order for dim in group[::turn]] for turn in (1, -1)] for order in orders
        ]
        self.count = width // BLOCK
        self.used = self.count * (self.count + 1) // 2 * BLOCK
        self.half = self.used // 2
        second = int(self.half // 2 * SHARE) // TILE * TILE
        self.parts = [self.half // 2 - second, second]
        self.rows = self.used
        self.outputs = 8

    def swap(self, value):
        return lax.ppermute(value, AXES, [(i, i ^ 1) for i in range(self.devices)])

    def send(self, value, lane, step):
        masks = [self.orders[lane][half][step][0] for half in range(2)]
        return lax.ppermute(value, AXES, [(i, i ^ masks[i % 2]) for i in range(self.devices)])

    def block_row(self, i, j):
        return (i * self.count - i * (i - 1) // 2 + (j - i)) * BLOCK

    def shapes(self):
        return [
            jax.ShapeDtypeStruct((self.parts[lane], LANES), jnp.float32)
            for _ in range(2)
            for lane in range(2)
            for _ in range(2)
        ]

    def each_part(self, refs, packed, go):
        me = lax.axis_index("wide") * lax.axis_size("narrow") + lax.axis_index("narrow")
        for k, ref in enumerate(refs):
            other, lane, digit = k // 4, k // 2 % 2, k % 2
            half = (me + other) % 2
            sides = []
            for order in self.orders[lane]:
                side = me * 0 + digit
                for bit in order[0][1]:
                    side = side + me // bit
                sides.append(side % 2)
            side = sides[0] + half * (sides[1] - sides[0])
            size = self.parts[lane]
            start = half * self.half + 2 * lane * self.parts[0] + side * size
            go(ref, packed.at[pl.ds(pl.multiple_of(start, TILE), size)])


def gram_kernel(plan, x_ref, valid_ref, *refs):
    outs, (packed, sem) = refs[: plan.outputs], refs[plan.outputs :]
    count = plan.count
    mask = valid_ref[...].astype(jnp.float32)
    mask_half = mask.astype(jnp.bfloat16)
    number = jnp.sum(mask)
    sums = jnp.dot(
        jnp.broadcast_to(mask_half, (16, mask.shape[1])), x_ref[...], preferred_element_type=jnp.float32
    )
    row = lax.broadcasted_iota(jnp.int32, (BLOCK, LANES), 0)
    lane = lax.broadcasted_iota(jnp.int32, (BLOCK, LANES), 1)
    for i in range(0, count, 2):
        left = x_ref[:, i * BLOCK : (i + 2) * BLOCK].T * mask_half
        part = jnp.dot(left, x_ref[:, i * BLOCK :], preferred_element_type=jnp.float32)
        for a in range(2):
            for j in range(i + a, count):
                block = part[a * BLOCK : (a + 1) * BLOCK, (j - i) * BLOCK : (j - i + 1) * BLOCK]
                if j == i + a:
                    s = sums[0:1, j * BLOCK : (j + 1) * BLOCK]
                    turned = jnp.where(lane[0:1] == 0, pltpu.roll(s, 1, 1), number)
                    low = jnp.where(row == BLOCK - 1, s, turned)
                    block = jnp.where(row <= lane, block, low)
                start = plan.block_row(i + a, j)
                packed[start : start + BLOCK, :] = block
    if plan.rows > plan.used:
        packed[plan.used :, :] = jnp.zeros((plan.rows - plan.used, LANES), jnp.float32)

    plan.each_part(outs, packed, lambda out, rows: pltpu.make_async_copy(rows, out, sem).start())
    plan.each_part(outs, packed, lambda out, rows: pltpu.make_async_copy(rows, out, sem).wait())


def gram_pieces(plan, x, valid):
    return pl.pallas_call(
        functools.partial(gram_kernel, plan),
        out_shape=plan.shapes(),
        in_specs=[pl.BlockSpec(memory_space=pltpu.VMEM)] * 2,
        out_specs=[pl.BlockSpec(memory_space=pl.ANY)] * plan.outputs,
        scratch_shapes=[pltpu.VMEM((plan.rows, LANES), jnp.float32), pltpu.SemaphoreType.DMA],
        compiler_params=pltpu.CompilerParams(vmem_limit_bytes=24 << 20),
        name="gram",
    )(x, valid.reshape(1, -1))


def whiten_kernel(plan, x_ref, *refs):
    pieces = refs[: plan.outputs]
    o_ref, packed, high, low, value, half_a, rest_a, half_b, rest_b, sem = refs[plan.outputs :]
    count = plan.count
    width = x_ref.shape[1]

    plan.each_part(pieces, packed, lambda piece, rows: pltpu.make_async_copy(piece, rows, sem).start())
    plan.each_part(pieces, packed, lambda piece, rows: pltpu.make_async_copy(piece, rows, sem).wait())

    row = lax.broadcasted_iota(jnp.int32, (BLOCK, LANES), 0)
    lane = lax.broadcasted_iota(jnp.int32, (BLOCK, LANES), 1)
    number = packed[BLOCK - 2 : BLOCK - 1, 1:2]
    inverse = 1.0 / number
    centers, columns = [], []
    for i in range(count):
        start = plan.block_row(i, i)
        last = packed[start + BLOCK - 1 : start + BLOCK, :]
        turned = pltpu.roll(packed[start + BLOCK - 2 : start + BLOCK - 1, :], LANES - 1, 1)
        center = jnp.where(lane[0:1] < LANES - 1, last, turned) * inverse
        centers.append(center)
        columns.append(jnp.broadcast_to(center, (BLOCK, LANES)).T)

    def split(cov):
        top = cov.astype(jnp.bfloat16)
        return top, (cov - top.astype(jnp.float32)).astype(jnp.bfloat16)

    trace = jnp.zeros((BLOCK, LANES), jnp.float32)
    square_diag = jnp.zeros((BLOCK, LANES), jnp.float32)
    square_off = jnp.zeros((BLOCK, LANES), jnp.float32)
    for i in range(count):
        for j in range(i, count):
            start = plan.block_row(i, j)
            block = packed[start : start + BLOCK, :]
            if i == j:
                block = jnp.where(row <= lane, block, block.T)
            cov = block * inverse - columns[i] * centers[j]
            if i == j:
                trace += jnp.where(row == lane, cov, 0.0)
                square_diag += cov * cov
            else:
                square_off += cov * cov
            rows, cols = pl.ds(i * BLOCK, BLOCK), pl.ds(j * BLOCK, BLOCK)
            high[rows, cols], low[rows, cols] = split(cov)
            if i != j:
                high[cols, rows], low[cols, rows] = split(cov.T)
    trace = jnp.sum(trace)
    square = jnp.sum(square_diag + 2.0 * square_off)
    ridge = 0.05 * trace / width + 1e-06
    norm = jnp.sqrt(jnp.full((1, 1), square + 2.0 * ridge * trace + width * ridge * ridge, jnp.float32))
    unit = 1.0 / norm
    final = 1.0 / (16.0 * jnp.sqrt(norm))

    step = 2 * BLOCK
    for j in range(count // 2):
        cols = pl.ds(j * step, step)
        center = jnp.concatenate(centers[2 * j : 2 * j + 2], axis=1)
        y = x_ref[:, cols].astype(jnp.float32) - center
        value[:, cols] = y
        half_a[:, cols], rest_a[:, cols] = split(y)

    halves = [(half_a, rest_a), (half_b, rest_b)]
    for k, weight in enumerate((-9.0, 27.0, -39.0, 36.0)):
        (half, rest), (half_next, rest_next) = halves[k % 2], halves[1 - k % 2]
        for j in range(count // 2):
            cols = pl.ds(j * step, step)
            center = jnp.concatenate(centers[2 * j : 2 * j + 2], axis=1)
            product = (
                jnp.dot(half[...], high[:, cols], preferred_element_type=jnp.float32)
                + jnp.dot(half[...], low[:, cols], preferred_element_type=jnp.float32)
                + jnp.dot(rest[...], high[:, cols], preferred_element_type=jnp.float32)
            )
            y = x_ref[:, cols].astype(jnp.float32) - center
            new = (product + ridge * value[:, cols]) * unit + weight * y
            if k < 3:
                value[:, cols] = new
                half_next[:, cols], rest_next[:, cols] = split(new)
            else:
                o_ref[:, cols] = (new * final).astype(jnp.bfloat16)


def whiten(plan, x, pieces):
    rows, width = x.shape
    half = pltpu.VMEM((rows, width), jnp.bfloat16)
    return pl.pallas_call(
        functools.partial(whiten_kernel, plan),
        out_shape=jax.ShapeDtypeStruct(x.shape, jnp.bfloat16),
        in_specs=[pl.BlockSpec(memory_space=pltpu.VMEM)] + [pl.BlockSpec(memory_space=pl.ANY)] * plan.outputs,
        out_specs=pl.BlockSpec(memory_space=pltpu.VMEM),
        scratch_shapes=[
            pltpu.VMEM((plan.rows, LANES), jnp.float32),
            pltpu.VMEM((width, width), jnp.bfloat16),
            pltpu.VMEM((width, width), jnp.bfloat16),
            pltpu.VMEM((rows, width), jnp.float32),
            half,
            half,
            half,
            half,
            pltpu.SemaphoreType.DMA,
        ],
        compiler_params=pltpu.CompilerParams(vmem_limit_bytes=40 << 20),
        name="whiten",
    )(x, *pieces)


def on_device(plan, embeddings, valid):
    parts = gram_pieces(plan, embeddings, valid)
    steps = len(plan.orders[0][0])
    total = [[], []]
    for digit in (1, 0):
        for lane in range(2):
            k = 2 * lane + digit
            total[lane].insert(0, parts[k] + plan.swap(parts[4 + k]))
    total = [total[lane][0] + plan.send(total[lane][1], lane, 0) for lane in range(2)]
    for step in range(1, steps):
        total = [total[lane] + plan.send(total[lane], lane, step) for lane in range(2)]
    near = [[total[lane], plan.send(total[lane], lane, 0)] for lane in range(2)]
    near = near[0] + near[1]
    return whiten(plan, embeddings, near + [plan.swap(part) for part in near])


def solution(mesh):
    spec = P(AXES, None)

    def program(embeddings, valid):
        plan = Plan(mesh, embeddings.shape[1])
        body = functools.partial(on_device, plan)
        return jax.shard_map(
            body, mesh=mesh, in_specs=(spec, P(AXES)), out_specs=spec, check_vma=False
        )(embeddings, valid)

    return program
```

```python
import functools

import jax
import jax.numpy as jnp
from jax import lax
from jax.experimental import pallas as pl
from jax.experimental.pallas import tpu as pltpu
from jax.sharding import PartitionSpec as P

AXES = ("wide", "narrow")
BLOCK = 128
LANES = 128
TILE = 8
SHARE = 0.5
EXACT_FROM = 2


class Plan:
    def __init__(self, mesh, width):
        wide, narrow = mesh.shape["wide"], mesh.shape["narrow"]
        self.devices = wide * narrow
        narrow_bits = [1 << k for k in range(1, narrow.bit_length() - 1)]
        wide_bits = [narrow << k for k in range(wide.bit_length() - 1)]
        first, second = wide_bits[0], narrow_bits[0]
        rest = wide_bits[1:] + narrow_bits[1:]
        self.orders = [[first, rest[0], second] + rest[1:], [second, rest[0], first] + rest[1:]]
        self.count = width // BLOCK
        self.used = self.count * (self.count + 1) // 2 * BLOCK
        self.half = self.used // 2
        late = int(self.half * SHARE) // (8 * TILE) * TILE
        self.chunks = [self.half // 8 - late, late]

    def swap(self, value):
        return lax.ppermute(value, AXES, [(i, i ^ 1) for i in range(self.devices)])

    def send(self, value, step):
        masks = [order[step] for order in self.orders]
        return lax.ppermute(value, AXES, [(i, i ^ masks[i % 2]) for i in range(self.devices)])

    def block_row(self, i, j):
        return (i * self.count - i * (i - 1) // 2 + (j - i)) * BLOCK

    def slots(self):
        me = lax.axis_index("wide") * lax.axis_size("narrow") + lax.axis_index("narrow")
        found, start = [], 0
        for half in range(2):
            other = (me + half) % 2
            sides = [(me // bit) % 2 for bit in self.orders[half][:3]]
            for lane in range(2):
                size = self.chunks[lane]
                for place in range(8):
                    slot = me * 0
                    for k in range(3):
                        slot = slot * 2 + (sides[k] + (place >> (2 - k))) % 2
                    where = other * self.half + 8 * lane * self.chunks[0] + slot * size
                    found.append((start, size, where))
                    start += size
        return found

    def runs(self, slots, start):
        found = []
        for first, size, where in slots:
            low, high = max(start, first), min(start + BLOCK, first + size)
            if low < high:
                found.append((low - start, high - low, pl.multiple_of(where + (low - first), TILE)))
        return found


def gram_kernel(plan, x_ref, valid_ref, packed):
    slots = plan.slots()
    count = plan.count
    mask = valid_ref[...].astype(jnp.float32)
    mask_half = mask.astype(jnp.bfloat16)
    number = jnp.sum(mask)
    sums = jnp.dot(
        jnp.broadcast_to(mask_half, (16, mask.shape[1])), x_ref[...], preferred_element_type=jnp.float32
    )
    row = lax.broadcasted_iota(jnp.int32, (BLOCK, LANES), 0)
    lane = lax.broadcasted_iota(jnp.int32, (BLOCK, LANES), 1)
    for i in range(0, count, 2):
        left = x_ref[:, i * BLOCK : (i + 2) * BLOCK].T * mask_half
        part = jnp.dot(left, x_ref[:, i * BLOCK :], preferred_element_type=jnp.float32)
        for a in range(2):
            for j in range(i + a, count):
                block = part[a * BLOCK : (a + 1) * BLOCK, (j - i) * BLOCK : (j - i + 1) * BLOCK]
                if j == i + a:
                    s = sums[0:1, j * BLOCK : (j + 1) * BLOCK]
                    turned = jnp.where(lane[0:1] == 0, pltpu.roll(s, 1, 1), number)
                    low = jnp.where(row == BLOCK - 1, s, turned)
                    block = jnp.where(row <= lane, block, low)
                for low, rows, where in plan.runs(slots, plan.block_row(i + a, j)):
                    packed[pl.ds(where, rows), :] = block[low : low + rows]


def gram(plan, x, valid):
    return pl.pallas_call(
        functools.partial(gram_kernel, plan),
        out_shape=jax.ShapeDtypeStruct((plan.used, LANES), jnp.float32),
        in_specs=[pl.BlockSpec(memory_space=pltpu.VMEM)] * 2,
        out_specs=pl.BlockSpec(memory_space=pltpu.VMEM),
        compiler_params=pltpu.CompilerParams(vmem_limit_bytes=24 << 20),
        name="gram",
    )(x, valid.reshape(1, -1))


def whiten_kernel(plan, x_ref, packed, o_ref, high, low, value, half_a, half_b, rest_a, rest_b):
    count = plan.count
    width = x_ref.shape[1]
    slots = plan.slots()

    def load(i, j):
        runs = plan.runs(slots, plan.block_row(i, j))
        found = [packed[pl.ds(where, rows), :] for _, rows, where in runs]
        return found[0] if len(found) == 1 else jnp.concatenate(found, axis=0)

    row = lax.broadcasted_iota(jnp.int32, (BLOCK, LANES), 0)
    lane = lax.broadcasted_iota(jnp.int32, (BLOCK, LANES), 1)
    diagonal = [load(i, i) for i in range(count)]
    inverse = 1.0 / diagonal[0][BLOCK - 2 : BLOCK - 1, 1:2]
    centers, columns = [], []
    for i in range(count):
        turned = pltpu.roll(diagonal[i][BLOCK - 2 : BLOCK - 1, :], LANES - 1, 1)
        center = jnp.where(lane[0:1] < LANES - 1, diagonal[i][BLOCK - 1 :, :], turned) * inverse
        centers.append(center)
        columns.append(jnp.broadcast_to(center, (BLOCK, LANES)).T)

    def split(cov):
        top = cov.astype(jnp.bfloat16)
        return top, (cov - top.astype(jnp.float32)).astype(jnp.bfloat16)

    trace = jnp.zeros((BLOCK, LANES), jnp.float32)
    square_diag = jnp.zeros((BLOCK, LANES), jnp.float32)
    square_off = jnp.zeros((BLOCK, LANES), jnp.float32)
    for i in range(count):
        for j in range(i, count):
            block = load(i, j)
            if i == j:
                block = jnp.where(row <= lane, block, block.T)
            cov = block * inverse - columns[i] * centers[j]
            if i == j:
                trace += jnp.where(row == lane, cov, 0.0)
                square_diag += cov * cov
            else:
                square_off += cov * cov
            rows, cols = pl.ds(i * BLOCK, BLOCK), pl.ds(j * BLOCK, BLOCK)
            high[rows, cols], low[rows, cols] = split(cov)
            if i != j:
                high[cols, rows], low[cols, rows] = split(cov.T)
    trace = jnp.sum(trace)
    square = jnp.sum(square_diag + 2.0 * square_off)
    ridge = 0.05 * trace / width + 1e-06
    norm = jnp.sqrt(jnp.full((1, 1), square + 2.0 * ridge * trace + width * ridge * ridge, jnp.float32))
    unit = 1.0 / norm
    final = 1.0 / (16.0 * jnp.sqrt(norm))

    step = 2 * BLOCK

    def shifted(j):
        center = jnp.concatenate(centers[2 * j : 2 * j + 2], axis=1)
        return x_ref[:, pl.ds(j * step, step)].astype(jnp.float32) - center

    for j in range(count // 2):
        half_a[:, pl.ds(j * step, step)] = shifted(j).astype(jnp.bfloat16)

    halves = [(half_a, rest_a), (half_b, rest_b)]
    for k, weight in enumerate((6.0, 6.0, 8.0, 16.0)):
        (half, rest), (half_next, rest_next) = halves[k % 2], halves[1 - k % 2]
        for j in range(count // 2):
            cols = pl.ds(j * step, step)
            product = jnp.dot(half[...], high[:, cols], preferred_element_type=jnp.float32)
            if k >= EXACT_FROM:
                product += jnp.dot(half[...], low[:, cols], preferred_element_type=jnp.float32)
                product += jnp.dot(rest[...], high[:, cols], preferred_element_type=jnp.float32)
            y = shifted(j)
            old = y if k == 0 else value[:, cols]
            new = weight * y - (product + ridge * old) * unit
            if k > 0:
                new += old
            if k == 3:
                o_ref[:, cols] = (new * final).astype(jnp.bfloat16)
            else:
                value[:, cols] = new
                half_next[:, cols], next_low = split(new)
                if k + 1 >= EXACT_FROM:
                    rest_next[:, cols] = next_low


def whiten(plan, x, packed):
    rows, width = x.shape
    half = pltpu.VMEM((rows, width), jnp.bfloat16)
    return pl.pallas_call(
        functools.partial(whiten_kernel, plan),
        out_shape=jax.ShapeDtypeStruct(x.shape, jnp.bfloat16),
        in_specs=[pl.BlockSpec(memory_space=pltpu.VMEM)] * 2,
        out_specs=pl.BlockSpec(memory_space=pltpu.VMEM),
        scratch_shapes=[
            pltpu.VMEM((width, width), jnp.bfloat16),
            pltpu.VMEM((width, width), jnp.bfloat16),
            pltpu.VMEM((rows, width), jnp.float32),
            half,
            half,
            half,
            half,
        ],
        compiler_params=pltpu.CompilerParams(vmem_limit_bytes=40 << 20),
        name="whiten",
    )(x, packed)


def after(value, earlier):
    return value if earlier is None else lax.optimization_barrier((value, earlier))[0]


def on_device(plan, embeddings, valid):
    packed = gram(plan, embeddings, valid)
    near, far = [], []
    for lane in range(2):
        span = 4 * plan.chunks[lane]
        starts = [half * plan.half + 8 * lane * plan.chunks[0] + k * span for half in range(2) for k in range(2)]
        parts = [packed[start : start + span] for start in starts]
        far.append(parts[1] + plan.swap(parts[3]))
        near.append(parts[0] + plan.swap(parts[2]))
    total, sent = near, None
    steps = len(plan.orders[0])
    for turn, step in enumerate(list(range(steps)) + [2, 1, 0]):
        for lane in range(2):
            t = total[lane]
            if turn == 0:
                out, kept = far[lane], t
            elif turn < 3:
                out, kept = t[t.shape[0] // 2 :], t[: t.shape[0] // 2]
            else:
                out, kept = t, t
            out = after(out, sent)
            sent = out
            got = plan.send(out, step)
            if turn < steps:
                total[lane] = kept + got
            elif step > 0:
                total[lane] = jnp.concatenate([kept, got], axis=0)
            else:
                total[lane] = [kept, got]
    near = total[0] + total[1]
    return whiten(plan, embeddings, jnp.concatenate(near + [plan.swap(part) for part in near], axis=0))


def solution(mesh):
    spec = P(AXES, None)

    def program(embeddings, valid):
        plan = Plan(mesh, embeddings.shape[1])
        body = functools.partial(on_device, plan)
        return jax.shard_map(
            body, mesh=mesh, in_specs=(spec, P(AXES)), out_specs=spec, check_vma=False
        )(embeddings, valid)

    return program
```

```python
import functools

import jax
import jax.numpy as jnp
from jax import lax
from jax.experimental import pallas as pl
from jax.experimental.pallas import tpu as pltpu
from jax.sharding import PartitionSpec as P

AXES = ("wide", "narrow")
BLOCK = 128
LANES = 128
TILE = 8
EXACT_FROM = 2


class Lane:
    def __init__(self, eighths, scatter, double, gather):
        self.eighths, self.scatter, self.double, self.gather = eighths, scatter, double, gather
        self.path = scatter + double + gather


class Plan:
    def __init__(self, mesh, width):
        wide, narrow = mesh.shape["wide"], mesh.shape["narrow"]
        self.devices = wide * narrow
        narrow_bits = [1 << k for k in range(1, narrow.bit_length() - 1)]
        wide_bits = [narrow << k for k in range(wide.bit_length() - 1)]
        p, q = (wide_bits[0], narrow_bits[0]), (narrow_bits[0], wide_bits[0])
        z, *rest = [(bit, bit) for bit in wide_bits[1:] + narrow_bits[1:]]
        self.lanes = [Lane(0.45, [z, q, p], rest, [p, q, z]), Lane(0, [p, q, z], rest, [z, q, p])]
        self.count = width // BLOCK
        self.used = self.count * (self.count + 1) // 2 * BLOCK
        self.half = self.used // 2
        unit = self.half // 8 // TILE
        self.sizes = [int(unit * 8 * lane.eighths + 0.5) >> len(lane.scatter) for lane in self.lanes[:-1]]
        self.sizes = [size * TILE << len(lane.scatter) for size, lane in zip(self.sizes, self.lanes)]
        self.sizes.append(self.half - sum(self.sizes))
        self.bases = [sum(self.sizes[:k]) for k in range(len(self.sizes))]

    def swap(self, value):
        return lax.ppermute(value, AXES, [(i, i ^ 1) for i in range(self.devices)])

    def send(self, value, bits):
        return lax.ppermute(value, AXES, [(i, i ^ bits[i % 2]) for i in range(self.devices)])

    def block_row(self, i, j):
        return (i * self.count - i * (i - 1) // 2 + (j - i)) * BLOCK

    def slots(self, gathered):
        me = lax.axis_index("wide") * lax.axis_size("narrow") + lax.axis_index("narrow")
        found, start = [], 0
        for half in range(2):
            other = (me + half) % 2
            for lane, total, base in zip(self.lanes, self.sizes, self.bases):
                depth = len(lane.scatter)
                size = total >> depth
                held = lane.gather[::-1] if gathered else lane.scatter
                for place in range(1 << depth):
                    slot = me * 0
                    for bits in held:
                        side = (place >> (depth - 1 - lane.scatter.index(bits))) % 2
                        slot = slot * 2 + (me // bits[half] + side) % 2
                    found.append((start, size, other * self.half + base + slot * size))
                    start += size
        return found

    def runs(self, slots, start):
        found = []
        for first, size, where in slots:
            low, high = max(start, first), min(start + BLOCK, first + size)
            if low < high:
                found.append((low - start, high - low, pl.multiple_of(where + (low - first), TILE)))
        return found


def gram_kernel(plan, x_hbm, valid_hbm, packed, x_ref, valid_ref, sems):
    count = plan.count
    step = 2 * BLOCK
    copies = [pltpu.make_async_copy(valid_hbm, valid_ref, sems.at[count // 2])]
    for i in reversed(range(count // 2)):
        cols = pl.ds(i * step, step)
        copies.append(pltpu.make_async_copy(x_hbm.at[:, cols], x_ref.at[:, cols], sems.at[i]))
    for copy in copies:
        copy.start()
    slots = plan.slots(False)
    row = lax.broadcasted_iota(jnp.int32, (BLOCK, LANES), 0)
    lane = lax.broadcasted_iota(jnp.int32, (BLOCK, LANES), 1)
    copies[0].wait()
    mask = valid_ref[...].astype(jnp.float32)
    mask_half = mask.astype(jnp.bfloat16)
    number = jnp.sum(mask)
    for copy, i in zip(copies[1:], reversed(range(0, count, 2))):
        copy.wait()
        here = x_ref[:, i * BLOCK : (i + 2) * BLOCK]
        sums = jnp.dot(
            jnp.broadcast_to(mask_half, (16, mask.shape[1])), here, preferred_element_type=jnp.float32
        )
        part = jnp.dot(here.T * mask_half, x_ref[:, i * BLOCK :], preferred_element_type=jnp.float32)
        for a in range(2):
            for j in range(i + a, count):
                block = part[a * BLOCK : (a + 1) * BLOCK, (j - i) * BLOCK : (j - i + 1) * BLOCK]
                if j == i + a:
                    s = sums[0:1, a * BLOCK : (a + 1) * BLOCK]
                    turned = jnp.where(lane[0:1] == 0, pltpu.roll(s, 1, 1), number)
                    low = jnp.where(row == BLOCK - 1, s, turned)
                    block = jnp.where(row <= lane, block, low)
                for low, rows, where in plan.runs(slots, plan.block_row(i + a, j)):
                    packed[pl.ds(where, rows), :] = block[low : low + rows]


def gram(plan, x, valid):
    return pl.pallas_call(
        functools.partial(gram_kernel, plan),
        out_shape=jax.ShapeDtypeStruct((plan.used, LANES), jnp.float32),
        in_specs=[pl.BlockSpec(memory_space=pltpu.HBM)] * 2,
        out_specs=pl.BlockSpec(memory_space=pltpu.VMEM),
        scratch_shapes=[
            pltpu.VMEM(x.shape, x.dtype),
            pltpu.VMEM((1, valid.shape[0]), valid.dtype),
            pltpu.SemaphoreType.DMA((plan.count // 2 + 1,)),
        ],
        compiler_params=pltpu.CompilerParams(vmem_limit_bytes=24 << 20),
        name="gram",
    )(*(pltpu.with_memory_space_constraint(a, pltpu.HBM) for a in (x, valid.reshape(1, -1))))


def whiten_kernel(plan, x_ref, packed, o_ref, high, low, value, half_a, half_b, rest_a, rest_b):
    count = plan.count
    width = x_ref.shape[1]
    slots = plan.slots(False)

    def load(i, j):
        runs = plan.runs(slots, plan.block_row(i, j))
        found = [packed[pl.ds(where, rows), :] for _, rows, where in runs]
        return found[0] if len(found) == 1 else jnp.concatenate(found, axis=0)

    row = lax.broadcasted_iota(jnp.int32, (BLOCK, LANES), 0)
    lane = lax.broadcasted_iota(jnp.int32, (BLOCK, LANES), 1)
    diagonal = [load(i, i) for i in range(count)]
    inverse = 1.0 / diagonal[0][BLOCK - 2 : BLOCK - 1, 1:2]
    centers, columns = [], []
    for i in range(count):
        turned = pltpu.roll(diagonal[i][BLOCK - 2 : BLOCK - 1, :], LANES - 1, 1)
        center = jnp.where(lane[0:1] < LANES - 1, diagonal[i][BLOCK - 1 :, :], turned) * inverse
        centers.append(center)
        columns.append(jnp.broadcast_to(center, (BLOCK, LANES)).T)

    def split(cov):
        top = cov.astype(jnp.bfloat16)
        return top, (cov - top.astype(jnp.float32)).astype(jnp.bfloat16)

    trace = jnp.zeros((BLOCK, LANES), jnp.float32)
    square_diag = jnp.zeros((BLOCK, LANES), jnp.float32)
    square_off = jnp.zeros((BLOCK, LANES), jnp.float32)
    for i in range(count):
        for j in range(i, count):
            block = load(i, j)
            if i == j:
                block = jnp.where(row <= lane, block, block.T)
            cov = block * inverse - columns[i] * centers[j]
            if i == j:
                trace += jnp.where(row == lane, cov, 0.0)
                square_diag += cov * cov
            else:
                square_off += cov * cov
            rows, cols = pl.ds(i * BLOCK, BLOCK), pl.ds(j * BLOCK, BLOCK)
            high[rows, cols], low[rows, cols] = split(cov)
            if i != j:
                high[cols, rows], low[cols, rows] = split(cov.T)
    trace = jnp.sum(trace)
    square = jnp.sum(square_diag + 2.0 * square_off)
    ridge = 0.05 * trace / width + 1e-06
    norm = jnp.sqrt(jnp.full((1, 1), square + 2.0 * ridge * trace + width * ridge * ridge, jnp.float32))
    unit = 1.0 / norm
    final = 1.0 / (16.0 * jnp.sqrt(norm))

    step = 2 * BLOCK

    def shifted(j):
        center = jnp.concatenate(centers[2 * j : 2 * j + 2], axis=1)
        return x_ref[:, pl.ds(j * step, step)].astype(jnp.float32) - center

    for j in range(count // 2):
        half_a[:, pl.ds(j * step, step)] = shifted(j).astype(jnp.bfloat16)

    halves = [(half_a, rest_a), (half_b, rest_b)]
    for k, weight in enumerate((6.0, 6.0, 8.0, 16.0)):
        (half, rest), (half_next, rest_next) = halves[k % 2], halves[1 - k % 2]
        for j in range(count // 2):
            cols = pl.ds(j * step, step)
            product = jnp.dot(half[...], high[:, cols], preferred_element_type=jnp.float32)
            if k >= EXACT_FROM:
                product += jnp.dot(half[...], low[:, cols], preferred_element_type=jnp.float32)
                product += jnp.dot(rest[...], high[:, cols], preferred_element_type=jnp.float32)
            y = shifted(j)
            old = y if k == 0 else value[:, cols]
            new = weight * y - (product + ridge * old) * unit
            if k > 0:
                new += old
            if k == 3:
                o_ref[:, cols] = (new * final).astype(jnp.bfloat16)
            else:
                value[:, cols] = new
                half_next[:, cols], next_low = split(new)
                if k + 1 >= EXACT_FROM:
                    rest_next[:, cols] = next_low


def whiten(plan, x, packed):
    rows, width = x.shape
    half = pltpu.VMEM((rows, width), jnp.bfloat16)
    return pl.pallas_call(
        functools.partial(whiten_kernel, plan),
        out_shape=jax.ShapeDtypeStruct(x.shape, jnp.bfloat16),
        in_specs=[pl.BlockSpec(memory_space=pltpu.VMEM)] * 2,
        out_specs=pl.BlockSpec(memory_space=pltpu.VMEM),
        scratch_shapes=[
            pltpu.VMEM((width, width), jnp.bfloat16),
            pltpu.VMEM((width, width), jnp.bfloat16),
            pltpu.VMEM((rows, width), jnp.float32),
            half,
            half,
            half,
            half,
        ],
        compiler_params=pltpu.CompilerParams(vmem_limit_bytes=40 << 20),
        name="whiten",
    )(x, packed)


def after(value, earlier):
    return value if earlier is None else lax.optimization_barrier((value, earlier))[0]


def on_device(plan, embeddings, valid):
    packed = gram(plan, embeddings, valid)
    total, far, sent = [], [], None
    for size, base in zip(plan.sizes, plan.bases):
        parts = [packed[start : start + size // 2] for k in range(2) for start in
                 (k * plan.half + base, k * plan.half + base + size // 2)]
        got = plan.swap(parts[3])
        sent = parts[1] + after(got, sent)
        far.append(sent)
        total.append((parts[0], parts[2]))
    ready = [(out, held) for out, held in zip(far, total)]
    sent = None
    for turn in range(max(len(lane.path) for lane in plan.lanes)):
        for k, lane in enumerate(plan.lanes):
            if turn >= len(lane.path):
                continue
            depth, (out, held) = len(lane.scatter), ready[k]
            out = after(out, sent)
            sent = out
            got = plan.send(out, lane.path[turn])
            if turn == 0:
                held = held[0] + plan.swap(held[1])
            if turn + 1 == len(lane.path):
                total[k] = [out, got]
                continue
            if turn < depth + len(lane.double):
                next_out = held + got
            else:
                next_out = jnp.concatenate([held, got], axis=0)
            if turn + 1 < depth:
                cut = next_out.shape[0] // 2
                ready[k] = (next_out[cut:], next_out[:cut])
            else:
                ready[k] = (next_out, next_out)
    near = [part for parts in total for part in parts]
    return whiten(plan, embeddings, jnp.concatenate(near + [plan.swap(part) for part in near], axis=0))


def solution(mesh):
    spec = P(AXES, None)

    def program(embeddings, valid):
        plan = Plan(mesh, embeddings.shape[1])

        def body(embeddings, valid):
            return on_device(plan, embeddings, valid)

        step = jax.shard_map(body, mesh=mesh, in_specs=(spec, P(AXES)), out_specs=spec, check_vma=False)
        return step(embeddings, valid)

    return program
```

```python
import functools

import jax
import jax.numpy as jnp
from jax import lax
from jax.experimental import pallas as pl
from jax.experimental.pallas import tpu as pltpu
from jax.sharding import PartitionSpec as P

AXES = ("wide", "narrow")
BLOCK = 128
LANES = 128
TILE = 8
EXACT_FROM = 2


class Lane:
    def __init__(self, eighths, scatter, double, gather):
        self.eighths, self.scatter, self.double, self.gather = eighths, scatter, double, gather
        self.path = scatter + double + gather


class Plan:
    def __init__(self, mesh, width):
        wide, narrow = mesh.shape["wide"], mesh.shape["narrow"]
        self.devices = wide * narrow
        narrow_bits = [1 << k for k in range(1, narrow.bit_length() - 1)]
        wide_bits = [narrow << k for k in range(wide.bit_length() - 1)]
        p, q = (wide_bits[0], narrow_bits[0]), (narrow_bits[0], wide_bits[0])
        z, *rest = [(bit, bit) for bit in wide_bits[1:] + narrow_bits[1:]]
        self.lanes = [Lane(0.472, [z, q, p], rest, [p, q, z]), Lane(0, [p, q, z], rest, [z, q, p])]
        self.count = width // BLOCK
        self.used = self.count * (self.count + 1) // 2 * BLOCK
        self.half = self.used // 2
        unit = self.half // 8 // TILE
        self.sizes = [int(unit * 8 * lane.eighths + 0.5) >> len(lane.scatter) for lane in self.lanes[:-1]]
        self.sizes = [size * TILE << len(lane.scatter) for size, lane in zip(self.sizes, self.lanes)]
        self.sizes.append(self.half - sum(self.sizes))
        self.bases = [sum(self.sizes[:k]) for k in range(len(self.sizes))]

    def swap(self, value):
        return lax.ppermute(value, AXES, [(i, i ^ 1) for i in range(self.devices)])

    def send(self, value, bits):
        return lax.ppermute(value, AXES, [(i, i ^ bits[i % 2]) for i in range(self.devices)])

    def block_row(self, i, j):
        return (i * self.count - i * (i - 1) // 2 + (j - i)) * BLOCK

    def slots(self, gathered):
        me = lax.axis_index("wide") * lax.axis_size("narrow") + lax.axis_index("narrow")
        found, start = [], 0
        for half in range(2):
            other = (me + half) % 2
            for lane, total, base in zip(self.lanes, self.sizes, self.bases):
                depth = len(lane.scatter)
                size = total >> depth
                held = lane.gather[::-1] if gathered else lane.scatter
                for place in range(1 << depth):
                    slot = me * 0
                    for bits in held:
                        side = (place >> (depth - 1 - lane.scatter.index(bits))) % 2
                        slot = slot * 2 + (me // bits[half] + side) % 2
                    found.append((start, size, other * self.half + base + slot * size))
                    start += size
        return found

    def runs(self, slots, start):
        found = []
        for first, size, where in slots:
            low, high = max(start, first), min(start + BLOCK, first + size)
            if low < high:
                found.append((low - start, high - low, pl.multiple_of(where + (low - first), TILE)))
        return found


def gram_kernel(plan, x_hbm, valid_hbm, packed, x_ref, valid_ref, sems):
    count = plan.count
    step = 2 * BLOCK
    copies = [pltpu.make_async_copy(valid_hbm, valid_ref, sems.at[count // 2])]
    for i in reversed(range(count // 2)):
        cols = pl.ds(i * step, step)
        copies.append(pltpu.make_async_copy(x_hbm.at[:, cols], x_ref.at[:, cols], sems.at[i]))
    for copy in copies:
        copy.start()
    slots = plan.slots(False)
    row = lax.broadcasted_iota(jnp.int32, (BLOCK, LANES), 0)
    lane = lax.broadcasted_iota(jnp.int32, (BLOCK, LANES), 1)
    copies[0].wait()
    mask = valid_ref[...].astype(jnp.float32)
    mask_half = mask.astype(jnp.bfloat16)
    number = jnp.sum(mask)
    for copy, i in zip(copies[1:], reversed(range(0, count, 2))):
        copy.wait()
        here = x_ref[:, i * BLOCK : (i + 2) * BLOCK]
        sums = jnp.dot(
            jnp.broadcast_to(mask_half, (16, mask.shape[1])), here, preferred_element_type=jnp.float32
        )
        part = jnp.dot(here.T * mask_half, x_ref[:, i * BLOCK :], preferred_element_type=jnp.float32)
        for a in range(2):
            for j in range(i + a, count):
                block = part[a * BLOCK : (a + 1) * BLOCK, (j - i) * BLOCK : (j - i + 1) * BLOCK]
                if j == i + a:
                    s = sums[0:1, a * BLOCK : (a + 1) * BLOCK]
                    turned = jnp.where(lane[0:1] == 0, pltpu.roll(s, 1, 1), number)
                    low = jnp.where(row == BLOCK - 1, s, turned)
                    block = jnp.where(row <= lane, block, low)
                for low, rows, where in plan.runs(slots, plan.block_row(i + a, j)):
                    packed[pl.ds(where, rows), :] = block[low : low + rows]


def gram(plan, x, valid):
    return pl.pallas_call(
        functools.partial(gram_kernel, plan),
        out_shape=jax.ShapeDtypeStruct((plan.used, LANES), jnp.float32),
        in_specs=[pl.BlockSpec(memory_space=pltpu.HBM)] * 2,
        out_specs=pl.BlockSpec(memory_space=pltpu.VMEM),
        scratch_shapes=[
            pltpu.VMEM(x.shape, x.dtype),
            pltpu.VMEM((1, valid.shape[0]), valid.dtype),
            pltpu.SemaphoreType.DMA((plan.count // 2 + 1,)),
        ],
        compiler_params=pltpu.CompilerParams(vmem_limit_bytes=24 << 20),
        name="gram",
    )(*(pltpu.with_memory_space_constraint(a, pltpu.HBM) for a in (x, valid.reshape(1, -1))))


def whiten_kernel(plan, x_ref, packed, out, high, low, value, half_a, half_b, rest_a, rest_b, o_ref, sem):
    count = plan.count
    width = x_ref.shape[1]
    slots = plan.slots(False)

    def load(i, j):
        runs = plan.runs(slots, plan.block_row(i, j))
        found = [packed[pl.ds(where, rows), :] for _, rows, where in runs]
        return found[0] if len(found) == 1 else jnp.concatenate(found, axis=0)

    row = lax.broadcasted_iota(jnp.int32, (BLOCK, LANES), 0)
    lane = lax.broadcasted_iota(jnp.int32, (BLOCK, LANES), 1)
    diagonal = [load(i, i) for i in range(count)]
    inverse = 1.0 / diagonal[0][BLOCK - 2 : BLOCK - 1, 1:2]
    centers, columns = [], []
    for i in range(count):
        turned = pltpu.roll(diagonal[i][BLOCK - 2 : BLOCK - 1, :], LANES - 1, 1)
        center = jnp.where(lane[0:1] < LANES - 1, diagonal[i][BLOCK - 1 :, :], turned) * inverse
        centers.append(center)
        columns.append(jnp.broadcast_to(center, (BLOCK, LANES)).T)

    def split(cov):
        top = cov.astype(jnp.bfloat16)
        return top, (cov - top.astype(jnp.float32)).astype(jnp.bfloat16)

    step = 2 * BLOCK

    def shifted(j):
        center = jnp.concatenate(centers[2 * j : 2 * j + 2], axis=1)
        return x_ref[:, pl.ds(j * step, step)].astype(jnp.float32) - center

    for j in range(count // 2):
        half_a[:, pl.ds(j * step, step)] = shifted(j).astype(jnp.bfloat16)

    trace = jnp.zeros((BLOCK, LANES), jnp.float32)
    square_diag = jnp.zeros((BLOCK, LANES), jnp.float32)
    square_off = jnp.zeros((BLOCK, LANES), jnp.float32)
    for i in range(count):
        for j in range(i, count):
            block = load(i, j)
            if i == j:
                block = jnp.where(row <= lane, block, block.T)
            cov = block * inverse - columns[i] * centers[j]
            if i == j:
                trace += jnp.where(row == lane, cov, 0.0)
                square_diag += cov * cov
            else:
                square_off += cov * cov
            rows, cols = pl.ds(i * BLOCK, BLOCK), pl.ds(j * BLOCK, BLOCK)
            high[rows, cols], low[rows, cols] = split(cov)
            if i != j:
                high[cols, rows], low[cols, rows] = split(cov.T)
        if i % 2:
            cols = pl.ds((i - 1) * BLOCK, step)
            value[:, cols] = jnp.dot(half_a[...], high[:, cols], preferred_element_type=jnp.float32)
    trace = jnp.sum(trace)
    square = jnp.sum(square_diag + 2.0 * square_off)
    ridge = 0.05 * trace / width + 1e-06
    norm = jnp.sqrt(jnp.full((1, 1), square + 2.0 * ridge * trace + width * ridge * ridge, jnp.float32))
    unit = 1.0 / norm
    final = 1.0 / (16.0 * jnp.sqrt(norm))

    halves = [(half_a, rest_a), (half_b, rest_b)]
    for k, weight in enumerate((6.0, 6.0, 8.0, 16.0)):
        (half, rest), (half_next, rest_next) = halves[k % 2], halves[1 - k % 2]
        for j in range(count // 2):
            cols = pl.ds(j * step, step)
            if k == 0:
                product = value[:, cols]
            elif k >= EXACT_FROM:
                both = jnp.dot(
                    jnp.concatenate([half[...], rest[...]], axis=0), high[:, cols], preferred_element_type=jnp.float32
                )
                product = both[: half.shape[0]] + both[half.shape[0] :]
                product += jnp.dot(half[...], low[:, cols], preferred_element_type=jnp.float32)
            else:
                product = jnp.dot(half[...], high[:, cols], preferred_element_type=jnp.float32)
            y = shifted(j)
            old = y if k == 0 else value[:, cols]
            new = weight * y - (product + ridge * old) * unit
            if k > 0:
                new += old
            if k == 3:
                o_ref[:, cols] = (new * final).astype(jnp.bfloat16)
                pltpu.make_async_copy(o_ref.at[:, cols], out.at[:, cols], sem.at[j]).start()
            else:
                value[:, cols] = new
                half_next[:, cols], next_low = split(new)
                if k + 1 >= EXACT_FROM:
                    rest_next[:, cols] = next_low
    for j in range(count // 2):
        cols = pl.ds(j * step, step)
        pltpu.make_async_copy(o_ref.at[:, cols], out.at[:, cols], sem.at[j]).wait()


def whiten(plan, x, packed):
    rows, width = x.shape
    half = pltpu.VMEM((rows, width), jnp.bfloat16)
    return pl.pallas_call(
        functools.partial(whiten_kernel, plan),
        out_shape=jax.ShapeDtypeStruct(x.shape, jnp.bfloat16),
        in_specs=[pl.BlockSpec(memory_space=pltpu.VMEM)] * 2,
        out_specs=pl.BlockSpec(memory_space=pl.ANY),
        scratch_shapes=[
            pltpu.VMEM((width, width), jnp.bfloat16),
            pltpu.VMEM((width, width), jnp.bfloat16),
            pltpu.VMEM((rows, width), jnp.float32),
            half,
            half,
            half,
            half,
            half,
            pltpu.SemaphoreType.DMA((plan.count // 2,)),
        ],
        compiler_params=pltpu.CompilerParams(vmem_limit_bytes=40 << 20),
        name="whiten",
    )(x, packed)


def after(value, earlier):
    return value if earlier is None else lax.optimization_barrier((value, earlier))[0]


def on_device(plan, embeddings, valid):
    packed = gram(plan, embeddings, valid)
    total, far, sent = [], [], None
    for size, base in zip(plan.sizes, plan.bases):
        parts = [packed[start : start + size // 2] for k in range(2) for start in
                 (k * plan.half + base, k * plan.half + base + size // 2)]
        got = plan.swap(parts[3])
        sent = parts[1] + after(got, sent)
        far.append(sent)
        total.append((parts[0], parts[2]))
    ready = [(out, held) for out, held in zip(far, total)]
    sent = None
    for turn in range(max(len(lane.path) for lane in plan.lanes)):
        for k, lane in enumerate(plan.lanes):
            if turn >= len(lane.path):
                continue
            depth, (out, held) = len(lane.scatter), ready[k]
            out = after(out, sent)
            sent = out
            got = plan.send(out, lane.path[turn])
            if turn == 0:
                held = held[0] + plan.swap(after(held[1], out))
            if turn + 1 == len(lane.path):
                total[k] = [out, got]
                continue
            if turn < depth + len(lane.double):
                next_out = held + got
            else:
                next_out = jnp.concatenate([held, got], axis=0)
            if turn + 1 < depth:
                cut = next_out.shape[0] // 2
                ready[k] = (next_out[cut:], next_out[:cut])
            else:
                ready[k] = (next_out, next_out)
    near = [part for parts in total for part in parts]
    return whiten(plan, embeddings, jnp.concatenate(near + [plan.swap(part) for part in near], axis=0))


def solution(mesh):
    spec = P(AXES, None)

    def program(embeddings, valid):
        plan = Plan(mesh, embeddings.shape[1])

        def body(embeddings, valid):
            return on_device(plan, embeddings, valid)

        step = jax.shard_map(body, mesh=mesh, in_specs=(spec, P(AXES)), out_specs=spec, check_vma=False)
        return step(embeddings, valid)

    return program
```
